256 devices in a mesh: dom: 64 (over x, z, core), ang: 4 (over y).
Axes of the slice: x: 4, y: 4, z: 8, core: 2. Of those that a mesh axis runs over, the one named last changes fastest.
Arguments:
- incident: bfloat16 [1024, 2, 64, 512], P('dom', None, 'ang'), may hold values from -6 to 6
- response: bfloat16 [1024, 2, 512, 512], P('dom', None, None, 'ang'), may hold values from -0.25 to 0.25
- jitter: int32 [1024], P('dom'), may hold values from 0 to 63
- block_cols: int32 [512, 12], P('dom'), may hold values from 0 to 511, as said below
- block_counts: int32 [512], P('dom'), may hold values from 1 to 12
- green_blocks: bfloat16 [512, 12, 2, 128, 128], P('dom'), may hold values from -0.15625 to 0.15625
Outputs:
- near_field: float32 [2, 64, 65536], P(None, 'ang', 'dom')
The draws below stay inside these ranges and needn't reach their ends.
Inputs may be any that keep to these rules, and one draw needn't show every extreme that they name: `block_cols`: block row r lies on device r // 8 of dom; every column block it names lies on a device at most 3 away along dom, and that distance is reached in every draw by a live entry.
All inputs are finite; a program needn't handle non-finite values.
Results may differ from the reference program's by a relative error of at most 0.0041.
Values may be sent and summed in bfloat16 or wider, within the bound.
No kernel may reach another device: no remote copies, remote signals or barrier semaphores. Data moves between devices by JAX's collectives and lax.ppermute only.
A program may use at most 64 MiB of HBM per device.

```python
import jax
import jax.numpy as jnp
from jax import lax

W = 512
STRIDE = 64
ANGLES = 64
GB = 128
MAXNZ = 12
REACH = 3
DOM_DEV = 16
DOMAINS = 1024
NS = 65536
BPD = 8
NBLK = 512
N_DOM = 64


def draw_block_cols(key, part):
    devices_dom = NBLK // BPD
    first_key, second_key = jax.random.split(key)
    owners = jnp.arange(NBLK, dtype=jnp.int32) // BPD
    distance = jax.random.randint(first_key, (NBLK, MAXNZ), -REACH, REACH + 1)
    sources = jnp.clip(owners[:, None] + distance, 0, devices_dom - 1)
    inside = jax.random.randint(second_key, (NBLK, MAXNZ), 0, BPD)
    columns = sources * BPD + inside
    columns = columns.at[0, 0].set(REACH * BPD + inside[0, 0])
    columns = columns.at[NBLK - 1, 0].set((devices_dom - 1 - REACH) * BPD + inside[NBLK - 1, 0])
    return columns.astype(jnp.int32)


def set_ends(entries, key, smallest, top_value):
    longest = entries.shape.index(max(entries.shape))
    spots = []
    for shift in (0, 1):
        where = [jax.random.randint(jax.random.fold_in(key, axis), (), 0, length) for axis, length in enumerate(entries.shape)]
        where[longest] = (where[longest] + shift) % entries.shape[longest]
        spots.append(tuple(where))
    return entries.at[spots[0]].set(smallest).at[spots[1]].set(top_value)


def block_scale(key, dims, cuts, smallest, high):
    def one(axis_at, blocks):
        draws = jax.random.uniform(jax.random.fold_in(jax.random.fold_in(key, 6), axis_at), (blocks,), jnp.float32, smallest / len(cuts), high / len(cuts))
        return jnp.repeat(jnp.exp(draws), dims[axis_at] // blocks).reshape((-1,) + (1,) * (len(dims) - axis_at - 1))

    factor_of = one(*cuts[0])
    for cut in cuts[1:]:
        factor_of = factor_of * one(*cut)
    return factor_of


def bell_draw(rng, shape, deviation, limit, shards=(), kind=jnp.bfloat16):
    array = jax.random.normal(rng, shape, jnp.float32) * deviation
    if len(shards) > 0:
        array = block_scale(rng, shape, shards, -0.22, 0.18) * array
    return jnp.clip(array, min=-limit, max=limit).astype(kind)


def setup_inputs(seed: int = 0) -> dict:
    streams_of = jax.random.split(jax.random.key(seed), 7)
    incident = bell_draw(streams_of[0], (DOMAINS, 2, ANGLES, W), 1.0, 6.0, ((0, 64), (2, 4)))
    response = bell_draw(streams_of[1], (DOMAINS, 2, W, W), W ** -0.5, 0.25, ((0, 64), (3, 4)))
    jitter = set_ends(jax.random.randint(streams_of[2], (DOMAINS,), 0, STRIDE), jax.random.fold_in(streams_of[2], 1), 0, STRIDE - 1).astype(jnp.int32)
    block_cols = draw_block_cols(jax.random.fold_in(streams_of[6], 71), 0)
    block_counts = set_ends(jax.random.randint(streams_of[4], (NBLK,), 1, MAXNZ + 1), jax.random.fold_in(streams_of[4], 1), 1, MAXNZ).astype(jnp.int32)
    green_blocks = bell_draw(streams_of[5], (NBLK, MAXNZ, 2, GB, GB), (GB * MAXNZ) ** -0.5, 0.15625, ((0, 64),))
    return dict(incident=incident, response=response, jitter=jitter, block_cols=block_cols, block_counts=block_counts, green_blocks=green_blocks)


def respond(incoming, panels):
    inc_re = incoming[:, 0].astype(jnp.float32)
    inc_im = incoming[:, 1].astype(jnp.float32)
    pan_re = panels[:, 0].astype(jnp.float32)
    pan_im = panels[:, 1].astype(jnp.float32)
    real_part = jnp.einsum('dan,dnc->dac', inc_re, pan_re) - jnp.einsum('dan,dnc->dac', inc_im, pan_im)
    imag_part = jnp.einsum('dan,dnc->dac', inc_re, pan_im) + jnp.einsum('dan,dnc->dac', inc_im, pan_re)
    return jnp.stack([real_part, imag_part], 1).astype(jnp.bfloat16)


def place(fields, starts, length):
    def single(field, first_col):
        empty = jnp.zeros((2, field.shape[1], length), jnp.float32)
        return lax.dynamic_update_slice(empty, field.astype(jnp.float32), (jnp.int32(0), jnp.int32(0), first_col.astype(jnp.int32)))
    return jax.vmap(single)(fields, starts)


def intersection_add(placed, stride):
    number = placed.shape[0]
    angle_rows = placed.shape[2]
    parts = placed.shape[3] // stride
    pieces = placed.reshape(number, 2, angle_rows, parts, stride)
    summed = jnp.zeros((number + parts - 1, 2, angle_rows, stride), jnp.float32)
    for part_index in range(parts):
        summed = summed.at[part_index:part_index + number].add(pieces[:, :, :, part_index])
    return jnp.transpose(summed, (1, 2, 0, 3)).reshape(2, angle_rows, (number + parts - 1) * stride)


def couple(blocks, cols, counts, green):
    picked = jnp.take(blocks, cols, axis=2)
    live = lax.broadcasted_iota(jnp.int32, cols.shape, 1) < counts[:, None]
    picked = jnp.where(live[None, None, :, :, None], picked, jnp.zeros((), picked.dtype))
    pick_re = picked[0].astype(jnp.float32)
    pick_im = picked[1].astype(jnp.float32)
    green_re = green[:, :, 0].astype(jnp.float32)
    green_im = green[:, :, 1].astype(jnp.float32)
    real_part = jnp.einsum('arkp,rkpq->arq', pick_re, green_re) - jnp.einsum('arkp,rkpq->arq', pick_im, green_im)
    imag_part = jnp.einsum('arkp,rkpq->arq', pick_re, green_im) + jnp.einsum('arkp,rkpq->arq', pick_im, green_re)
    return jnp.stack([real_part, imag_part], 0)


def reference(incident, response, jitter, block_cols, block_counts, green_blocks):
    grouped = (incident.reshape(N_DOM, DOM_DEV, 2, ANGLES, W), response.reshape(N_DOM, DOM_DEV, 2, W, W))
    fields = lax.map(lambda pair: respond(pair[0], pair[1]), grouped).reshape(DOMAINS, 2, ANGLES, W)
    plane = intersection_add(place(fields, jitter, W + STRIDE), STRIDE)[:, :, :NS]
    stitched = plane.astype(jnp.bfloat16)
    blocks = stitched.reshape(2, ANGLES, NBLK, GB)
    rows_grouped = (block_cols.reshape(N_DOM, BPD, MAXNZ), block_counts.reshape(N_DOM, BPD), green_blocks.reshape(N_DOM, BPD, MAXNZ, 2, GB, GB))
    coupled = lax.map(lambda item: couple(blocks, item[0], item[1], item[2]), rows_grouped)
    return jnp.transpose(coupled, (1, 2, 0, 3, 4)).reshape(2, ANGLES, NS)
```

```python
import functools

import jax
import jax.numpy as jnp
from jax import lax
from jax.experimental import pallas as pl
from jax.experimental.pallas import tpu as pltpu
from jax.sharding import PartitionSpec as P

LANES = 128
REACH = 3
VMEM = pl.BlockSpec(memory_space=pltpu.VMEM)
SMEM = pl.BlockSpec(memory_space=pltpu.SMEM)


def ring(block, distance):
    size = lax.axis_size("ang")
    return lax.ppermute(block, "ang", [(i, (i + distance) % size) for i in range(size)])


def to_next_domains(block, distance):
    doms, angs = lax.axis_size("dom"), lax.axis_size("ang")
    route = [
        (d * angs + a, (d + 1) * angs + (a + distance) % angs) for d in range(doms - 1) for a in range(angs)
    ]
    return lax.ppermute(block, ("dom", "ang"), route)


def facing(block, even_step):
    doms = lax.axis_size("dom")
    route = [(i, i + (even_step if i % 2 == 0 else -even_step)) for i in range(doms)]
    return lax.ppermute(block, "dom", [(s, t) for s, t in route if 0 <= t < doms])


def placed_sums(jitter_ref, pieces, response_ref):
    domains = response_ref.shape[0]
    per_piece = domains // len(pieces)
    angles = pieces[0].shape[2]
    sums = [None] * (domains // 2 + 1)
    for d in range(domains):
        wave = pieces[d // per_piece][d % per_piece].reshape(2 * angles, -1)
        panel = jnp.concatenate([response_ref[d, 0], response_ref[d, 1]], axis=1)
        product = jnp.dot(wave, panel, preferred_element_type=jnp.float32)
        real = product[:angles, :LANES] - product[angles:, LANES:]
        imag = product[:angles, LANES:] + product[angles:, :LANES]
        field = jnp.concatenate([real, imag], axis=0).astype(jnp.bfloat16).astype(jnp.float32)
        start = (d % 2) * (LANES // 2) + jitter_ref[d]
        turned = pltpu.roll(field, start, 1)
        lane = lax.broadcasted_iota(jnp.int32, turned.shape, 1)
        here = jnp.where(lane >= start, turned, 0.0)
        after = turned - here
        for block, part in ((d // 2, here), (d // 2 + 1, after)):
            sums[block] = part if sums[block] is None else sums[block] + part
    return sums


def respond_kernel(groups, halves, *refs):
    jitter_ref, response_ref = refs[0], refs[1]
    inputs = refs[2 : 2 + groups * halves]
    outputs = refs[2 + groups * halves :]
    for g in range(groups):
        sums = placed_sums(jitter_ref, inputs[g * halves : (g + 1) * halves], response_ref)
        main_ref, halo_ref = outputs[2 * g], outputs[2 * g + 1]
        for b in range(main_ref.shape[0]):
            main_ref[b] = sums[b].astype(main_ref.dtype)
        first = len(sums) - halo_ref.shape[0]
        for b in range(halo_ref.shape[0]):
            halo_ref[b] = sums[first + b].astype(halo_ref.dtype)


def respond(jitter, response, groups, main_type):
    domains, _, depth, cols = response.shape
    halves = len(groups[0])
    angles = groups[0][0].shape[2]
    main = jax.ShapeDtypeStruct((domains // 2, 2 * angles, LANES), main_type)
    halo = jax.ShapeDtypeStruct((4, 2 * angles, LANES), jnp.bfloat16)
    flops = len(groups) * domains * 2 * (2 * angles) * depth * (2 * cols)
    return pl.pallas_call(
        functools.partial(respond_kernel, len(groups), halves),
        out_shape=[main, halo] * len(groups),
        in_specs=[SMEM, VMEM] + [VMEM] * (len(groups) * halves),
        out_specs=[VMEM] * (2 * len(groups)),
        compiler_params=pltpu.CompilerParams(vmem_limit_bytes=24 * 2**20),
        cost_estimate=pl.CostEstimate(flops=flops, bytes_accessed=response.size * 2, transcendentals=0),
        name="respond",
    )(jitter, response, *[piece for group in groups for piece in group])


def stitch_kernel(*refs):
    mains, halos, (out_ref, plane, edge) = refs[:4], refs[4:8], refs[8:]
    me = lax.axis_index("ang")
    blocks = out_ref.shape[0]
    plane[...] = jnp.zeros_like(plane)
    edge[...] = jnp.zeros_like(edge)
    for step in range(4):
        owner = lax.rem(me + step, 4)
        plane[pl.ds(owner, blocks)] += mains[step][...].astype(jnp.float32)
        edge[pl.ds(owner, 4)] += halos[step][...].astype(jnp.float32)
    plane[pl.ds(0, 4)] += edge[pl.ds(3, 4)]
    out_ref[...] = plane[pl.ds(0, blocks)].astype(out_ref.dtype)


def stitch(mains, halos):
    blocks, rows, lanes = mains[0].shape
    return pl.pallas_call(
        stitch_kernel,
        out_shape=jax.ShapeDtypeStruct((blocks, rows, lanes), jnp.bfloat16),
        in_specs=[VMEM] * 8,
        out_specs=VMEM,
        scratch_shapes=[
            pltpu.VMEM((blocks + 4, rows, lanes), jnp.float32),
            pltpu.VMEM((8, rows, lanes), jnp.float32),
        ],
        compiler_params=pltpu.CompilerParams(vmem_limit_bytes=8 * 2**20),
        name="stitch",
    )(*mains, *halos)


def couple_kernel(cols_ref, counts_ref, green_ref, *refs):
    parts, out_ref, window = refs[:7], refs[7], refs[8]
    blocks, rows, lanes = parts[0].shape
    angles = rows // 2
    entries = green_ref.shape[1]
    for s in range(7):
        window[pl.ds(s * blocks, blocks)] = parts[s][...]
    dead = 7 * blocks
    window[dead] = jnp.zeros((rows, lanes), window.dtype)
    me = lax.axis_index("dom")
    odd = lax.rem(me, 2) == 1
    for r in range(green_ref.shape[0]):
        picked = []
        for k in range(entries):
            col = cols_ref[r, k]
            distance = col // blocks - me
            slot = jnp.where(odd, REACH - distance, REACH + distance)
            index = jnp.where(k < counts_ref[r], slot * blocks + col % blocks, dead)
            picked.append(window[index])
        wave = jnp.concatenate(picked, axis=1)
        green = jnp.concatenate(
            [green_ref[r, :, 0].reshape(entries * lanes, lanes), green_ref[r, :, 1].reshape(entries * lanes, lanes)],
            axis=1,
        )
        product = jnp.dot(wave, green, preferred_element_type=jnp.float32)
        at = pl.ds(r * lanes, lanes)
        out_ref[0, :, at] = product[:angles, :lanes] - product[angles:, lanes:]
        out_ref[1, :, at] = product[:angles, lanes:] + product[angles:, :lanes]


def couple(block_cols, block_counts, green, parts):
    rows_here, entries = block_cols.shape
    blocks, rows, lanes = parts[0].shape
    flops = rows_here * 2 * rows * entries * lanes * 2 * lanes
    return pl.pallas_call(
        couple_kernel,
        out_shape=jax.ShapeDtypeStruct((2, rows // 2, rows_here * lanes), jnp.float32),
        in_specs=[SMEM, SMEM, VMEM] + [VMEM] * 7,
        out_specs=VMEM,
        scratch_shapes=[pltpu.VMEM((7 * blocks + 8, rows, lanes), jnp.bfloat16)],
        compiler_params=pltpu.CompilerParams(vmem_limit_bytes=24 * 2**20),
        cost_estimate=pl.CostEstimate(flops=flops, bytes_accessed=green.size * 2, transcendentals=0),
        name="couple",
    )(block_cols, block_counts, green, *parts)


def per_device(incident, response, jitter, block_cols, block_counts, green_blocks):
    half = incident.shape[0] // 2
    low, high = incident[:half], incident[half:]
    before_low, after_high = ring(low, 1), ring(high, -1)
    before_high, after_low = ring(high, 1), ring(low, -1)
    across_low, across_high = ring(before_low, 1), ring(after_high, -1)

    own_main, own_halo = respond(jitter, response, [(incident,)], jnp.float32)
    before_main, before_halo, after_main, after_halo = respond(
        jitter, response, [(before_low, before_high), (after_low, after_high)], jnp.bfloat16
    )
    across_main, across_halo = respond(jitter, response, [(across_low, across_high)], jnp.bfloat16)

    mains = [own_main, ring(before_main, -1), ring(across_main, 2), ring(after_main, 1)]
    halos = [
        to_next_domains(own_halo, 0),
        to_next_domains(before_halo, -1),
        to_next_domains(across_halo, 2),
        to_next_domains(after_halo, 1),
    ]
    own = stitch(mains, halos)

    near = facing(own, -1)
    middle = facing(own, 2)
    far = facing(own, -3)
    other = facing(own, 1)
    other_near = facing(near, 1)
    other_middle = facing(middle, 1)
    return couple(block_cols, block_counts, green_blocks, [far, middle, near, own, other, other_near, other_middle])


def solution(mesh):
    return jax.shard_map(
        per_device,
        mesh=mesh,
        in_specs=(
            P("dom", None, "ang", None),
            P("dom", None, None, "ang"),
            P("dom"),
            P("dom", None),
            P("dom"),
            P("dom", None, None, None, None),
        ),
        out_specs=P(None, "ang", "dom"),
        check_vma=False,
    )
```

```python
import functools

import jax
import jax.numpy as jnp
from jax import lax
from jax.experimental import pallas as pl
from jax.experimental.pallas import tpu as pltpu
from jax.sharding import PartitionSpec as P

LANES = 128
REACH = 3
HALO = 4
VMEM = pl.BlockSpec(memory_space=pltpu.VMEM)
SMEM = pl.BlockSpec(memory_space=pltpu.SMEM)


def ring(block, distance):
    size = lax.axis_size("ang")
    return lax.ppermute(block, "ang", [(i, (i + distance) % size) for i in range(size)])


def facing(block, even_step):
    doms = lax.axis_size("dom")
    route = [(i, i + (even_step if i % 2 == 0 else -even_step)) for i in range(doms)]
    return lax.ppermute(block, "dom", [(s, t) for s, t in route if 0 <= t < doms])


def placed_sums(jitter_ref, pieces, response_ref):
    domains = response_ref.shape[0]
    per_piece = domains // len(pieces)
    angles = pieces[0].shape[2]
    sums = [None] * (domains // 2 + 1)
    for d in range(domains):
        wave = pieces[d // per_piece][d % per_piece].reshape(2 * angles, -1)
        panel = jnp.concatenate([response_ref[d, 0], response_ref[d, 1]], axis=1)
        product = jnp.dot(wave, panel, preferred_element_type=jnp.float32)
        real = product[:angles, :LANES] - product[angles:, LANES:]
        imag = product[:angles, LANES:] + product[angles:, :LANES]
        field = jnp.concatenate([real, imag], axis=0).astype(jnp.bfloat16).astype(jnp.float32)
        start = (d % 2) * (LANES // 2) + jitter_ref[d]
        turned = pltpu.roll(field, start, 1)
        lane = lax.broadcasted_iota(jnp.int32, turned.shape, 1)
        here = jnp.where(lane >= start, turned, 0.0)
        after = turned - here
        for block, part in ((d // 2, here), (d // 2 + 1, after)):
            sums[block] = part if sums[block] is None else sums[block] + part
    return sums


def own_kernel(chunk, jitter_ref, incident_hbm, response_hbm, sums_ref, response_ref, incident_ref, wave_sem, panel_sems):
    domains = response_ref.shape[0]
    wave_copy = pltpu.make_async_copy(incident_hbm, incident_ref, wave_sem)
    wave_copy.start()
    copies = []
    for c in range(domains // chunk):
        at = pl.ds(c * chunk, chunk)
        copies.append(pltpu.make_async_copy(response_hbm.at[at], response_ref.at[at], panel_sems.at[c]))
        copies[-1].start()
    wave_copy.wait()
    for copy in copies:
        copy.wait()
    sums = placed_sums(jitter_ref, [incident_ref], response_ref)
    for b, block in enumerate(sums):
        sums_ref[b] = block


def respond_own(jitter, incident, response):
    domains, _, depth, cols = response.shape
    angles = incident.shape[2]
    chunk = domains // 4
    hbm = pl.BlockSpec(memory_space=pltpu.HBM)
    return pl.pallas_call(
        functools.partial(own_kernel, chunk),
        out_shape=[
            jax.ShapeDtypeStruct((domains // 2 + 1, 2 * angles, LANES), jnp.float32),
            jax.ShapeDtypeStruct(response.shape, response.dtype),
        ],
        in_specs=[SMEM, hbm, hbm],
        out_specs=[VMEM, VMEM],
        scratch_shapes=[
            pltpu.VMEM(incident.shape, incident.dtype),
            pltpu.SemaphoreType.DMA,
            pltpu.SemaphoreType.DMA((domains // chunk,)),
        ],
        compiler_params=pltpu.CompilerParams(vmem_limit_bytes=16 * 2**20),
        cost_estimate=pl.CostEstimate(
            flops=domains * 8 * angles * depth * cols, bytes_accessed=4 * response.size, transcendentals=0
        ),
        name="respond_own",
    )(jitter, incident, response)


def respond_kernel(groups, halves, *refs):
    jitter_ref, response_ref = refs[0], refs[1]
    inputs = refs[2 : 2 + groups * halves]
    outputs = refs[2 + groups * halves :]
    for g in range(groups):
        sums = placed_sums(jitter_ref, inputs[g * halves : (g + 1) * halves], response_ref)
        for b, block in enumerate(sums):
            outputs[g][b] = block.astype(outputs[g].dtype)


def respond(jitter, response, groups):
    domains, _, depth, cols = response.shape
    halves = len(groups[0])
    angles = groups[0][0].shape[2]
    sums = jax.ShapeDtypeStruct((domains // 2 + 1, 2 * angles, LANES), jnp.bfloat16)
    return pl.pallas_call(
        functools.partial(respond_kernel, len(groups), halves),
        out_shape=[sums] * len(groups),
        in_specs=[SMEM, VMEM] + [VMEM] * (len(groups) * halves),
        out_specs=[VMEM] * len(groups),
        compiler_params=pltpu.CompilerParams(vmem_limit_bytes=16 * 2**20),
        cost_estimate=pl.CostEstimate(
            flops=len(groups) * domains * 8 * angles * depth * cols, bytes_accessed=2 * response.size, transcendentals=0
        ),
        name="respond",
    )(jitter, response, *[piece for group in groups for piece in group])


def stitch_kernel(*refs):
    sources, plane = refs[:4], refs[4]
    me = lax.axis_index("ang")
    plane[...] = jnp.zeros_like(plane)
    for step in range(4):
        owner = lax.rem(me + step, 4)
        plane[pl.ds(owner, sources[step].shape[0])] += sources[step][...].astype(jnp.float32)


def stitch(sources):
    blocks, rows, lanes = sources[0].shape
    return pl.pallas_call(
        stitch_kernel,
        out_shape=jax.ShapeDtypeStruct((blocks + 3, rows, lanes), jnp.float32),
        in_specs=[VMEM] * 4,
        out_specs=VMEM,
        compiler_params=pltpu.CompilerParams(vmem_limit_bytes=8 * 2**20),
        name="stitch",
    )(*sources)


def pack_kernel(mine_ref, other_ref, chip_ref, far_ref):
    odd = lax.rem(lax.axis_index("dom"), 2) == 1
    blocks = mine_ref.shape[0] - HALO

    def fill(even_ref, odd_ref, first):
        chip_ref[pl.ds(0, blocks)] = even_ref[pl.ds(0, blocks)].astype(chip_ref.dtype)
        joined = odd_ref[pl.ds(0, HALO)] + even_ref[pl.ds(blocks, HALO)]
        chip_ref[pl.ds(blocks, HALO)] = joined.astype(chip_ref.dtype)
        rest = odd_ref[pl.ds(HALO, blocks)]
        chip_ref[pl.ds(blocks + HALO, blocks)] = rest.astype(chip_ref.dtype)
        far_ref[...] = chip_ref[pl.ds(first, blocks + HALO)]

    @pl.when(odd)
    def _():
        fill(other_ref, mine_ref, blocks)

    @pl.when(jnp.logical_not(odd))
    def _():
        fill(mine_ref, other_ref, 0)


def pack(mine, other):
    total, rows, lanes = mine.shape
    blocks = total - HALO
    return pl.pallas_call(
        pack_kernel,
        out_shape=[
            jax.ShapeDtypeStruct((2 * blocks + HALO, rows, lanes), jnp.bfloat16),
            jax.ShapeDtypeStruct((blocks + HALO, rows, lanes), jnp.bfloat16),
        ],
        in_specs=[VMEM] * 2,
        out_specs=[VMEM] * 2,
        compiler_params=pltpu.CompilerParams(vmem_limit_bytes=8 * 2**20),
        name="pack",
    )(mine, other)


def couple_kernel(cols_ref, counts_ref, green_ref, chip_ref, near_ref, far_ref, swap_near_ref, swap_far_ref, out_ref, window):
    rows, lanes = chip_ref.shape[1:]
    blocks = far_ref.shape[0] - HALO
    angles = rows // 2
    entries = green_ref.shape[1]
    me = lax.axis_index("dom")
    odd = lax.rem(me, 2) == 1

    def put(slot, ref, first, halo_ref=None, halo_first=None):
        at = slot * blocks
        if halo_ref is None:
            window[pl.ds(at, blocks)] = ref[pl.ds(first, blocks)]
            return
        low = ref[pl.ds(first, HALO)].astype(jnp.float32)
        halo = halo_ref[pl.ds(halo_first, HALO)].astype(jnp.float32)
        window[pl.ds(at, HALO)] = (low + halo).astype(window.dtype)
        window[pl.ds(at + HALO, blocks - HALO)] = ref[pl.ds(first + HALO, blocks - HALO)]

    def fill(left_ref, right_ref, left_far_ref):
        put(1, left_ref, 0, left_far_ref, blocks)
        put(2, left_ref, blocks)
        put(3, chip_ref, 0, left_ref, 2 * blocks)
        put(4, chip_ref, blocks)
        put(5, right_ref, 0, chip_ref, 2 * blocks)
        put(6, right_ref, blocks)

    @pl.when(odd)
    def _():
        fill(swap_near_ref, near_ref, swap_far_ref)
        put(7, far_ref, 0, near_ref, 2 * blocks)

    @pl.when(jnp.logical_not(odd))
    def _():
        fill(near_ref, swap_near_ref, far_ref)
        put(0, far_ref, 0)

    dead = 8 * blocks
    window[dead] = jnp.zeros((rows, lanes), window.dtype)
    first_col = (me - lax.rem(me, 2) - REACH) * blocks
    for r in range(green_ref.shape[0]):
        picked = []
        for k in range(entries):
            index = jnp.where(k < counts_ref[r], cols_ref[r, k] - first_col, dead)
            picked.append(window[index])
        wave = jnp.concatenate(picked, axis=1)
        green = jnp.concatenate(
            [green_ref[r, :, 0].reshape(entries * lanes, lanes), green_ref[r, :, 1].reshape(entries * lanes, lanes)],
            axis=1,
        )
        product = jnp.dot(wave, green, preferred_element_type=jnp.float32)
        at = pl.ds(r * lanes, lanes)
        out_ref[0, :, at] = product[:angles, :lanes] - product[angles:, lanes:]
        out_ref[1, :, at] = product[:angles, lanes:] + product[angles:, :lanes]


def couple(block_cols, block_counts, green, chip, near, far, swap_near, swap_far):
    rows_here, entries = block_cols.shape
    _, rows, lanes = chip.shape
    blocks = far.shape[0] - HALO
    flops = rows_here * 2 * rows * entries * lanes * 2 * lanes
    return pl.pallas_call(
        couple_kernel,
        out_shape=jax.ShapeDtypeStruct((2, rows // 2, rows_here * lanes), jnp.float32),
        in_specs=[SMEM, SMEM] + [VMEM] * 6,
        out_specs=VMEM,
        scratch_shapes=[pltpu.VMEM((8 * blocks + 8, rows, lanes), jnp.bfloat16)],
        compiler_params=pltpu.CompilerParams(vmem_limit_bytes=24 * 2**20),
        cost_estimate=pl.CostEstimate(flops=flops, bytes_accessed=green.size * 2, transcendentals=0),
        name="couple",
    )(block_cols, block_counts, green, chip, near, far, swap_near, swap_far)


def per_device(incident, response, jitter, block_cols, block_counts, green_blocks):
    half = incident.shape[0] // 2
    low, high = incident[:half], incident[half:]
    before_low, after_high = ring(low, 1), ring(high, -1)
    before_high, after_low = ring(high, 1), ring(low, -1)
    across_low, across_high = ring(before_low, 1), ring(after_high, -1)

    own, panels = respond_own(jitter, incident, response)
    before, after = respond(jitter, panels, [(before_low, before_high), (after_low, after_high)])
    (across,) = respond(jitter, panels, [(across_low, across_high)])
    mine = stitch([own, ring(before, -1), ring(across, 2), ring(after, 1)])

    chip, far = pack(mine, facing(mine, 1))
    near_in, far_in = facing(chip, -1), facing(far, -3)
    return couple(
        block_cols, block_counts, green_blocks, chip, near_in, far_in, facing(near_in, 1), facing(far_in, 1)
    )


def solution(mesh):
    return jax.shard_map(
        per_device,
        mesh=mesh,
        in_specs=(
            P("dom", None, "ang", None),
            P("dom", None, None, "ang"),
            P("dom"),
            P("dom", None),
            P("dom"),
            P("dom", None, None, None, None),
        ),
        out_specs=P(None, "ang", "dom"),
        check_vma=False,
    )
```

```python
import functools

import jax
import jax.numpy as jnp
from jax import lax
from jax.experimental import pallas as pl
from jax.experimental.pallas import tpu as pltpu
from jax.sharding import PartitionSpec as P

LANES = 128
REACH = 3
HALO = 4
VMEM = pl.BlockSpec(memory_space=pltpu.VMEM)
SMEM = pl.BlockSpec(memory_space=pltpu.SMEM)


def ring(block, distance):
    size = lax.axis_size("ang")
    return lax.ppermute(block, "ang", [(i, (i + distance) % size) for i in range(size)])


def facing(block, even_step):
    doms = lax.axis_size("dom")
    route = [(i, i + (even_step if i % 2 == 0 else -even_step)) for i in range(doms)]
    return lax.ppermute(block, "dom", [(s, t) for s, t in route if 0 <= t < doms])


def placed_sums(jitter_ref, pieces, response_ref):
    domains = response_ref.shape[0]
    per_piece = domains // len(pieces)
    angles = pieces[0].shape[2]
    sums = [None] * (domains // 2 + 1)
    for d in range(domains):
        wave = pieces[d // per_piece][d % per_piece].reshape(2 * angles, -1)
        panel = jnp.concatenate([response_ref[d, 0], response_ref[d, 1]], axis=1)
        product = jnp.dot(wave, panel, preferred_element_type=jnp.float32)
        real = product[:angles, :LANES] - product[angles:, LANES:]
        imag = product[:angles, LANES:] + product[angles:, :LANES]
        field = jnp.concatenate([real, imag], axis=0).astype(jnp.bfloat16).astype(jnp.float32)
        start = (d % 2) * (LANES // 2) + jitter_ref[d]
        turned = pltpu.roll(field, start, 1)
        lane = lax.broadcasted_iota(jnp.int32, turned.shape, 1)
        here = jnp.where(lane >= start, turned, 0.0)
        after = turned - here
        for block, part in ((d // 2, here), (d // 2 + 1, after)):
            sums[block] = part if sums[block] is None else sums[block] + part
    return sums


def gate_kernel(held_ref, after_ref, out_ref):
    pass


def gate(held, after):
    return pl.pallas_call(
        gate_kernel,
        out_shape=jax.ShapeDtypeStruct(held.shape, held.dtype),
        in_specs=[VMEM, VMEM],
        out_specs=VMEM,
        input_output_aliases={0: 0},
        compiler_params=pltpu.CompilerParams(vmem_limit_bytes=2**20),
        name="gate",
    )(held, after)


def respond_kernel(groups, halves, *refs):
    jitter_ref, response_ref = refs[0], refs[1]
    inputs = refs[2 : 2 + groups * halves]
    outputs = refs[2 + groups * halves :]
    for g in range(groups):
        sums = placed_sums(jitter_ref, inputs[g * halves : (g + 1) * halves], response_ref)
        for b, block in enumerate(sums):
            outputs[g][b] = block.astype(outputs[g].dtype)


def respond(jitter, response, groups, kind=jnp.bfloat16):
    domains, _, depth, cols = response.shape
    halves = len(groups[0])
    angles = groups[0][0].shape[2]
    sums = jax.ShapeDtypeStruct((domains // 2 + 1, 2 * angles, LANES), kind)
    return pl.pallas_call(
        functools.partial(respond_kernel, len(groups), halves),
        out_shape=[sums] * len(groups),
        in_specs=[SMEM, VMEM] + [VMEM] * (len(groups) * halves),
        out_specs=[VMEM] * len(groups),
        compiler_params=pltpu.CompilerParams(vmem_limit_bytes=16 * 2**20),
        cost_estimate=pl.CostEstimate(
            flops=len(groups) * domains * 8 * angles * depth * cols, bytes_accessed=2 * response.size, transcendentals=0
        ),
        name="respond",
    )(jitter, response, *[piece for group in groups for piece in group])


def stitch_kernel(*refs):
    sources, plane = refs[:4], refs[4]
    me = lax.axis_index("ang")
    plane[...] = jnp.zeros_like(plane)
    for step in range(4):
        owner = lax.rem(me + step, 4)
        plane[pl.ds(owner, sources[step].shape[0])] += sources[step][...].astype(jnp.float32)


def stitch(sources):
    blocks, rows, lanes = sources[0].shape
    return pl.pallas_call(
        stitch_kernel,
        out_shape=jax.ShapeDtypeStruct((blocks + 3, rows, lanes), jnp.float32),
        in_specs=[VMEM] * 4,
        out_specs=VMEM,
        compiler_params=pltpu.CompilerParams(vmem_limit_bytes=8 * 2**20),
        name="stitch",
    )(*sources)


def pack_kernel(mine_ref, other_ref, chip_ref, far_ref):
    odd = lax.rem(lax.axis_index("dom"), 2) == 1
    blocks = mine_ref.shape[0] - HALO

    def fill(even_ref, odd_ref, first):
        chip_ref[pl.ds(0, blocks)] = even_ref[pl.ds(0, blocks)].astype(chip_ref.dtype)
        joined = odd_ref[pl.ds(0, HALO)] + even_ref[pl.ds(blocks, HALO)]
        chip_ref[pl.ds(blocks, HALO)] = joined.astype(chip_ref.dtype)
        rest = odd_ref[pl.ds(HALO, blocks)]
        chip_ref[pl.ds(blocks + HALO, blocks)] = rest.astype(chip_ref.dtype)
        far_ref[...] = chip_ref[pl.ds(first, blocks + HALO)]

    @pl.when(odd)
    def _():
        fill(other_ref, mine_ref, 0)

    @pl.when(jnp.logical_not(odd))
    def _():
        fill(mine_ref, other_ref, blocks)


def pack(mine, other):
    total, rows, lanes = mine.shape
    blocks = total - HALO
    return pl.pallas_call(
        pack_kernel,
        out_shape=[
            jax.ShapeDtypeStruct((2 * blocks + HALO, rows, lanes), jnp.bfloat16),
            jax.ShapeDtypeStruct((blocks + HALO, rows, lanes), jnp.bfloat16),
        ],
        in_specs=[VMEM] * 2,
        out_specs=[VMEM] * 2,
        compiler_params=pltpu.CompilerParams(vmem_limit_bytes=8 * 2**20),
        name="pack",
    )(mine, other)


def couple_kernel(cols_ref, counts_ref, green_ref, chip_ref, near_ref, far_ref, swap_near_ref, swap_far_ref, out_ref, window):
    rows, lanes = chip_ref.shape[1:]
    blocks = far_ref.shape[0] - HALO
    angles = rows // 2
    entries = green_ref.shape[1]
    me = lax.axis_index("dom")
    odd = lax.rem(me, 2) == 1

    def put(slot, ref, first, halo_ref=None, halo_first=None):
        at = slot * blocks
        if halo_ref is None:
            window[pl.ds(at, blocks)] = ref[pl.ds(first, blocks)]
            return
        low = ref[pl.ds(first, HALO)].astype(jnp.float32)
        halo = halo_ref[pl.ds(halo_first, HALO)].astype(jnp.float32)
        window[pl.ds(at, HALO)] = (low + halo).astype(window.dtype)
        window[pl.ds(at + HALO, blocks - HALO)] = ref[pl.ds(first + HALO, blocks - HALO)]

    def fill(left_ref, right_ref, left_far_ref):
        put(1, left_ref, 0, left_far_ref, blocks)
        put(2, left_ref, blocks)
        put(3, chip_ref, 0, left_ref, 2 * blocks)
        put(4, chip_ref, blocks)
        put(5, right_ref, 0, chip_ref, 2 * blocks)
        put(6, right_ref, blocks)

    @pl.when(odd)
    def _():
        fill(swap_near_ref, near_ref, swap_far_ref)
        put(7, far_ref, 0, near_ref, 2 * blocks)

    @pl.when(jnp.logical_not(odd))
    def _():
        fill(near_ref, swap_near_ref, far_ref)
        put(0, far_ref, 0)

    dead = 8 * blocks
    window[dead] = jnp.zeros((rows, lanes), window.dtype)
    first_col = (me - lax.rem(me, 2) - REACH) * blocks
    for r in range(green_ref.shape[0]):
        picked = []
        for k in range(entries):
            index = jnp.where(k < counts_ref[r], cols_ref[r, k] - first_col, dead)
            picked.append(window[index])
        wave = jnp.concatenate(picked, axis=1)
        green = jnp.concatenate(
            [green_ref[r, :, 0].reshape(entries * lanes, lanes), green_ref[r, :, 1].reshape(entries * lanes, lanes)],
            axis=1,
        )
        product = jnp.dot(wave, green, preferred_element_type=jnp.float32)
        at = pl.ds(r * lanes, lanes)
        out_ref[0, :, at] = product[:angles, :lanes] - product[angles:, lanes:]
        out_ref[1, :, at] = product[:angles, lanes:] + product[angles:, :lanes]


def couple(block_cols, block_counts, green, chip, near, far, swap_near, swap_far):
    rows_here, entries = block_cols.shape
    _, rows, lanes = chip.shape
    blocks = far.shape[0] - HALO
    flops = rows_here * 2 * rows * entries * lanes * 2 * lanes
    return pl.pallas_call(
        couple_kernel,
        out_shape=jax.ShapeDtypeStruct((2, rows // 2, rows_here * lanes), jnp.float32),
        in_specs=[SMEM, SMEM] + [VMEM] * 6,
        out_specs=VMEM,
        scratch_shapes=[pltpu.VMEM((8 * blocks + 8, rows, lanes), jnp.bfloat16)],
        compiler_params=pltpu.CompilerParams(vmem_limit_bytes=24 * 2**20),
        cost_estimate=pl.CostEstimate(flops=flops, bytes_accessed=green.size * 2, transcendentals=0),
        name="couple",
    )(block_cols, block_counts, green, chip, near, far, swap_near, swap_far)


def per_device(incident, response, jitter, block_cols, block_counts, green_blocks):
    half = incident.shape[0] // 2
    low, high = incident[:half], incident[half:]
    before_low, after_high = ring(low, 1), ring(high, -1)
    before_high, after_low = ring(high, 1), ring(low, -1)
    (own,) = respond(jitter, response, [(low, high)], jnp.float32)
    before_low, after_high = gate(before_low, own), gate(after_high, own)
    across_low, across_high = ring(before_low, 1), ring(after_high, -1)

    before, after = respond(jitter, response, [(before_low, before_high), (after_low, after_high)])
    (across,) = respond(jitter, response, [(across_low, across_high)])
    mine = stitch([own, ring(before, -1), ring(across, 2), ring(after, 1)])

    chip, far = pack(mine, facing(mine, 1))
    far_in, near_in = facing(far, 4), facing(chip, 2)
    return couple(
        block_cols, block_counts, green_blocks, chip, near_in, far_in, facing(near_in, 1), facing(far_in, 1)
    )


def solution(mesh):
    return jax.shard_map(
        per_device,
        mesh=mesh,
        in_specs=(
            P("dom", None, "ang", None),
            P("dom", None, None, "ang"),
            P("dom"),
            P("dom", None),
            P("dom"),
            P("dom", None, None, None, None),
        ),
        out_specs=P(None, "ang", "dom"),
        check_vma=False,
    )
```

```python
import functools

import jax
import jax.numpy as jnp
from jax import lax
from jax.experimental import pallas as pl
from jax.experimental.pallas import tpu as pltpu
from jax.sharding import PartitionSpec as P

LANES = 128
REACH = 3
HALO = 4
VMEM = pl.BlockSpec(memory_space=pltpu.VMEM)
SMEM = pl.BlockSpec(memory_space=pltpu.SMEM)


def angle_pairs(block, shift):
    size = lax.axis_size("ang")
    if shift == 2:
        return lax.ppermute(block, "ang", [(a, (a + 2) % size) for a in range(size)])
    return lax.ppermute(block, "ang", [(a, (((a + shift) ^ 1) - shift) % size) for a in range(size)])


def other_core(block):
    doms = lax.axis_size("dom")
    return lax.ppermute(block, "dom", [(i, i ^ 1) for i in range(doms)])


def pairs(block, distance):
    chips = lax.axis_size("dom") // 2
    route = []
    for i in range(2 * chips):
        chip, core = i // 2, i % 2
        partner = chip ^ distance if core == distance - 1 else ((chip + distance) ^ distance) - distance
        if 0 <= partner < chips:
            route.append((i, 2 * partner + core))
    return lax.ppermute(block, "dom", route)


def ahead(distance):
    me = lax.axis_index("dom")
    return lax.rem(me + distance - 1, 2) == lax.rem(me // (2 * distance), 2)


def placed_sums(jitter_ref, pieces, response_ref):
    domains = response_ref.shape[0]
    per_piece = domains // len(pieces)
    angles = pieces[0].shape[2]
    sums = [None] * (domains // 2 + 1)
    for d in range(domains):
        wave = pieces[d // per_piece][d % per_piece].reshape(2 * angles, -1)
        panel = jnp.concatenate([response_ref[d, 0], response_ref[d, 1]], axis=1)
        product = jnp.dot(wave, panel, preferred_element_type=jnp.float32)
        real = product[:angles, :LANES] - product[angles:, LANES:]
        imag = product[:angles, LANES:] + product[angles:, :LANES]
        field = jnp.concatenate([real, imag], axis=0).astype(jnp.bfloat16).astype(jnp.float32)
        start = (d % 2) * (LANES // 2) + jitter_ref[d]
        turned = pltpu.roll(field, start, 1)
        lane = lax.broadcasted_iota(jnp.int32, turned.shape, 1)
        here = jnp.where(lane >= start, turned, 0.0)
        after = turned - here
        for block, part in ((d // 2, here), (d // 2 + 1, after)):
            sums[block] = part if sums[block] is None else sums[block] + part
    return sums


def gate_kernel(held_ref, after_ref, out_ref):
    pass


def gate(held, after):
    return pl.pallas_call(
        gate_kernel,
        out_shape=jax.ShapeDtypeStruct(held.shape, held.dtype),
        in_specs=[VMEM, VMEM],
        out_specs=VMEM,
        input_output_aliases={0: 0},
        compiler_params=pltpu.CompilerParams(vmem_limit_bytes=2**20),
        name="gate",
    )(held, after)


def respond_kernel(groups, halves, *refs):
    jitter_ref, response_ref = refs[0], refs[1]
    inputs = refs[2 : 2 + groups * halves]
    outputs = refs[2 + groups * halves :]
    for g in range(groups):
        sums = placed_sums(jitter_ref, inputs[g * halves : (g + 1) * halves], response_ref)
        for b, block in enumerate(sums):
            outputs[g][b] = block.astype(outputs[g].dtype)


def respond(jitter, response, groups, kind=jnp.bfloat16):
    domains, _, depth, cols = response.shape
    halves = len(groups[0])
    angles = groups[0][0].shape[2]
    sums = jax.ShapeDtypeStruct((domains // 2 + 1, 2 * angles, LANES), kind)
    return pl.pallas_call(
        functools.partial(respond_kernel, len(groups), halves),
        out_shape=[sums] * len(groups),
        in_specs=[SMEM, VMEM] + [VMEM] * (len(groups) * halves),
        out_specs=[VMEM] * len(groups),
        compiler_params=pltpu.CompilerParams(vmem_limit_bytes=16 * 2**20),
        cost_estimate=pl.CostEstimate(
            flops=len(groups) * domains * 8 * angles * depth * cols, bytes_accessed=2 * response.size, transcendentals=0
        ),
        name="respond",
    )(jitter, response, *[piece for group in groups for piece in group])


def stitch_kernel(*refs):
    sources, plane = refs[:4], refs[4]
    me = lax.axis_index("ang")
    plane[...] = jnp.zeros_like(plane)
    side = jnp.where(lax.rem(me, 2) == 0, 1, 3)
    for step, owner in enumerate((me, lax.rem(me + side, 4), lax.rem(me + 4 - side, 4), lax.rem(me + 2, 4))):
        plane[pl.ds(owner, sources[step].shape[0])] += sources[step][...].astype(jnp.float32)


def stitch(sources):
    blocks, rows, lanes = sources[0].shape
    return pl.pallas_call(
        stitch_kernel,
        out_shape=jax.ShapeDtypeStruct((blocks + 3, rows, lanes), jnp.float32),
        in_specs=[VMEM] * 4,
        out_specs=VMEM,
        compiler_params=pltpu.CompilerParams(vmem_limit_bytes=8 * 2**20),
        name="stitch",
    )(*sources)


def pack_kernel(mine_ref, other_ref, chip_ref, far_ref):
    odd = lax.rem(lax.axis_index("dom"), 2) == 1
    blocks = mine_ref.shape[0] - HALO

    def fill(even_ref, odd_ref):
        chip_ref[pl.ds(0, blocks)] = even_ref[pl.ds(0, blocks)].astype(chip_ref.dtype)
        joined = odd_ref[pl.ds(0, HALO)] + even_ref[pl.ds(blocks, HALO)]
        chip_ref[pl.ds(blocks, HALO)] = joined.astype(chip_ref.dtype)
        rest = odd_ref[pl.ds(HALO, blocks)]
        chip_ref[pl.ds(blocks + HALO, blocks)] = rest.astype(chip_ref.dtype)

    @pl.when(odd)
    def _():
        fill(other_ref, mine_ref)

    @pl.when(jnp.logical_not(odd))
    def _():
        fill(mine_ref, other_ref)

    far_ref[...] = chip_ref[pl.ds(jnp.where(ahead(2), blocks, 0), blocks + HALO)]


def pack(mine, other):
    total, rows, lanes = mine.shape
    blocks = total - HALO
    return pl.pallas_call(
        pack_kernel,
        out_shape=[
            jax.ShapeDtypeStruct((2 * blocks + HALO, rows, lanes), jnp.bfloat16),
            jax.ShapeDtypeStruct((blocks + HALO, rows, lanes), jnp.bfloat16),
        ],
        in_specs=[VMEM] * 2,
        out_specs=[VMEM] * 2,
        compiler_params=pltpu.CompilerParams(vmem_limit_bytes=8 * 2**20),
        name="pack",
    )(mine, other)


def couple_kernel(cols_ref, counts_ref, green_ref, chip_ref, near_ref, far_ref, swap_near_ref, swap_far_ref, out_ref, window):
    rows, lanes = chip_ref.shape[1:]
    blocks = far_ref.shape[0] - HALO
    angles = rows // 2
    entries = green_ref.shape[1]
    me = lax.axis_index("dom")

    def put(slot, ref, first, halo_ref=None, halo_first=None):
        at = slot * blocks
        if halo_ref is None:
            window[pl.ds(at, blocks)] = ref[pl.ds(first, blocks)]
            return
        low = ref[pl.ds(first, HALO)].astype(jnp.float32)
        halo = halo_ref[pl.ds(halo_first, HALO)].astype(jnp.float32)
        window[pl.ds(at, HALO)] = (low + halo).astype(window.dtype)
        window[pl.ds(at + HALO, blocks - HALO)] = ref[pl.ds(first + HALO, blocks - HALO)]

    def fill(left_ref, right_ref, left_far_ref, right_far_ref):
        put(0, left_far_ref, 0)
        put(1, left_ref, 0, left_far_ref, blocks)
        put(2, left_ref, blocks)
        put(3, chip_ref, 0, left_ref, 2 * blocks)
        put(4, chip_ref, blocks)
        put(5, right_ref, 0, chip_ref, 2 * blocks)
        put(6, right_ref, blocks)
        put(7, right_far_ref, 0, right_ref, 2 * blocks)

    for near_ahead, sides in ((True, (swap_near_ref, near_ref)), (False, (near_ref, swap_near_ref))):
        for far_ahead, far_sides in ((True, (swap_far_ref, far_ref)), (False, (far_ref, swap_far_ref))):

            @pl.when(jnp.logical_and(ahead(1) == near_ahead, ahead(2) == far_ahead))
            def _(sides=sides, far_sides=far_sides):
                fill(*sides, *far_sides)

    dead = 8 * blocks
    window[dead] = jnp.zeros((rows, lanes), window.dtype)
    first_col = (me - lax.rem(me, 2) - REACH) * blocks
    for r in range(green_ref.shape[0]):
        picked = []
        for k in range(entries):
            index = jnp.where(k < counts_ref[r], cols_ref[r, k] - first_col, dead)
            picked.append(window[index])
        wave = jnp.concatenate(picked, axis=1)
        green = jnp.concatenate(
            [green_ref[r, :, 0].reshape(entries * lanes, lanes), green_ref[r, :, 1].reshape(entries * lanes, lanes)],
            axis=1,
        )
        product = jnp.dot(wave, green, preferred_element_type=jnp.float32)
        at = pl.ds(r * lanes, lanes)
        out_ref[0, :, at] = product[:angles, :lanes] - product[angles:, lanes:]
        out_ref[1, :, at] = product[:angles, lanes:] + product[angles:, :lanes]


def couple(block_cols, block_counts, green, chip, near, far, swap_near, swap_far):
    rows_here, entries = block_cols.shape
    _, rows, lanes = chip.shape
    blocks = far.shape[0] - HALO
    flops = rows_here * 2 * rows * entries * lanes * 2 * lanes
    return pl.pallas_call(
        couple_kernel,
        out_shape=jax.ShapeDtypeStruct((2, rows // 2, rows_here * lanes), jnp.float32),
        in_specs=[SMEM, SMEM] + [VMEM] * 6,
        out_specs=VMEM,
        scratch_shapes=[pltpu.VMEM((8 * blocks + 8, rows, lanes), jnp.bfloat16)],
        compiler_params=pltpu.CompilerParams(vmem_limit_bytes=24 * 2**20),
        cost_estimate=pl.CostEstimate(flops=flops, bytes_accessed=green.size * 2, transcendentals=0),
        name="couple",
    )(block_cols, block_counts, green, chip, near, far, swap_near, swap_far)


def per_device(incident, response, jitter, block_cols, block_counts, green_blocks):
    half = incident.shape[0] // 2
    low, high = incident[:half], incident[half:]
    one_low, two_high = angle_pairs(low, 0), angle_pairs(high, 1)
    one_high, two_low = angle_pairs(high, 0), angle_pairs(low, 1)
    (own,) = respond(jitter, response, [(low, high)], jnp.float32)
    one_low, two_high = gate(one_low, own), gate(two_high, own)
    across_low, across_high = angle_pairs(one_low, 1), angle_pairs(two_high, 0)

    one, two = respond(jitter, response, [(one_low, one_high), (two_low, two_high)])
    (across,) = respond(jitter, response, [(across_low, across_high)])
    mine = stitch([own, angle_pairs(one, 0), angle_pairs(two, 1), angle_pairs(across, 2)])

    chip, far = pack(mine, other_core(mine))
    near_in, far_in = pairs(chip, 1), pairs(far, 2)
    return couple(
        block_cols, block_counts, green_blocks, chip, near_in, far_in, other_core(near_in), other_core(far_in)
    )


def solution(mesh):
    return jax.shard_map(
        per_device,
        mesh=mesh,
        in_specs=(
            P("dom", None, "ang", None),
            P("dom", None, None, "ang"),
            P("dom"),
            P("dom", None),
            P("dom"),
            P("dom", None, None, None, None),
        ),
        out_specs=P(None, "ang", "dom"),
        check_vma=False,
    )
```

```python
import functools

import jax
import jax.numpy as jnp
from jax import lax
from jax.experimental import pallas as pl
from jax.experimental.pallas import tpu as pltpu
from jax.sharding import PartitionSpec as P

LANES = 128
REACH = 3
HALO = 4
VMEM = pl.BlockSpec(memory_space=pltpu.VMEM)
SMEM = pl.BlockSpec(memory_space=pltpu.SMEM)


def angle_pairs(block, shift):
    size = lax.axis_size("ang")
    if shift == 2:
        return lax.ppermute(block, "ang", [(a, (a + 2) % size) for a in range(size)])
    return lax.ppermute(block, "ang", [(a, (((a + shift) ^ 1) - shift) % size) for a in range(size)])


def other_core(block):
    doms = lax.axis_size("dom")
    return lax.ppermute(block, "dom", [(i, i ^ 1) for i in range(doms)])


def pairs(block, distance):
    chips = lax.axis_size("dom") // 2
    route = []
    for i in range(2 * chips):
        chip, core = i // 2, i % 2
        partner = chip ^ distance if core == distance - 1 else ((chip + distance) ^ distance) - distance
        if 0 <= partner < chips:
            route.append((i, 2 * partner + core))
    return lax.ppermute(block, "dom", route)


def ahead(distance):
    me = lax.axis_index("dom")
    return lax.rem(me + distance - 1, 2) == lax.rem(me // (2 * distance), 2)


def placed_sums(jitter_ref, pieces, response_ref):
    jitter = jitter_ref[...]
    domains = response_ref.shape[0]
    per_piece = domains // len(pieces)
    angles = pieces[0].shape[2]
    sums = [None] * (domains // 2 + 1)
    for d in range(domains):
        wave = pieces[d // per_piece][d % per_piece].reshape(2 * angles, -1)
        panel = jnp.concatenate([response_ref[d, 0], response_ref[d, 1]], axis=1)
        product = jnp.dot(wave, panel, preferred_element_type=jnp.float32)
        real = product[:angles, :LANES] - product[angles:, LANES:]
        imag = product[:angles, LANES:] + product[angles:, :LANES]
        field = jnp.concatenate([real, imag], axis=0).astype(jnp.bfloat16).astype(jnp.float32)
        start = (d % 2) * (LANES // 2) + jitter[0, d]
        turned = pltpu.roll(field, start, 1)
        lane = lax.broadcasted_iota(jnp.int32, turned.shape, 1)
        here = jnp.where(lane >= start, turned, 0.0)
        after = turned - here
        for block, part in ((d // 2, here), (d // 2 + 1, after)):
            sums[block] = part if sums[block] is None else sums[block] + part
    return sums


def gate_kernel(held_ref, after_ref, out_ref):
    pass


def gate(held, after):
    return pl.pallas_call(
        gate_kernel,
        out_shape=jax.ShapeDtypeStruct(held.shape, held.dtype),
        in_specs=[VMEM, VMEM],
        out_specs=VMEM,
        input_output_aliases={0: 0},
        compiler_params=pltpu.CompilerParams(vmem_limit_bytes=2**20),
        name="gate",
    )(held, after)


def respond_kernel(groups, halves, *refs):
    jitter_ref, response_ref = refs[0], refs[1]
    inputs = refs[2 : 2 + groups * halves]
    outputs = refs[2 + groups * halves :]
    for g in range(groups):
        sums = placed_sums(jitter_ref, inputs[g * halves : (g + 1) * halves], response_ref)
        for b, block in enumerate(sums):
            outputs[g][b] = block.astype(outputs[g].dtype)


def respond(jitter, response, groups, kind=jnp.bfloat16):
    domains, _, depth, cols = response.shape
    halves = len(groups[0])
    angles = groups[0][0].shape[2]
    sums = jax.ShapeDtypeStruct((domains // 2 + 1, 2 * angles, LANES), kind)
    return pl.pallas_call(
        functools.partial(respond_kernel, len(groups), halves),
        out_shape=[sums] * len(groups),
        in_specs=[VMEM, VMEM] + [VMEM] * (len(groups) * halves),
        out_specs=[VMEM] * len(groups),
        compiler_params=pltpu.CompilerParams(vmem_limit_bytes=16 * 2**20),
        cost_estimate=pl.CostEstimate(
            flops=len(groups) * domains * 8 * angles * depth * cols, bytes_accessed=2 * response.size, transcendentals=0
        ),
        name="respond",
    )(jitter[None], response, *[piece for group in groups for piece in group])


def stitch_kernel(*refs):
    sources, plane = refs[:4], refs[4]
    me = lax.axis_index("ang")
    plane[...] = jnp.zeros_like(plane)
    side = jnp.where(lax.rem(me, 2) == 0, 1, 3)
    for step, owner in enumerate((me, lax.rem(me + side, 4), lax.rem(me + 4 - side, 4), lax.rem(me + 2, 4))):
        plane[pl.ds(owner, sources[step].shape[0])] += sources[step][...].astype(jnp.float32)


def stitch(sources):
    blocks, rows, lanes = sources[0].shape
    return pl.pallas_call(
        stitch_kernel,
        out_shape=jax.ShapeDtypeStruct((blocks + 3, rows, lanes), jnp.float32),
        in_specs=[VMEM] * 4,
        out_specs=VMEM,
        compiler_params=pltpu.CompilerParams(vmem_limit_bytes=8 * 2**20),
        name="stitch",
    )(*sources)


def pack_kernel(mine_ref, other_ref, chip_ref, far_ref):
    odd = lax.rem(lax.axis_index("dom"), 2) == 1
    blocks = mine_ref.shape[0] - HALO

    def fill(even_ref, odd_ref):
        chip_ref[pl.ds(0, blocks)] = even_ref[pl.ds(0, blocks)].astype(chip_ref.dtype)
        joined = odd_ref[pl.ds(0, HALO)] + even_ref[pl.ds(blocks, HALO)]
        chip_ref[pl.ds(blocks, HALO)] = joined.astype(chip_ref.dtype)
        rest = odd_ref[pl.ds(HALO, blocks)]
        chip_ref[pl.ds(blocks + HALO, blocks)] = rest.astype(chip_ref.dtype)

    @pl.when(odd)
    def _():
        fill(other_ref, mine_ref)

    @pl.when(jnp.logical_not(odd))
    def _():
        fill(mine_ref, other_ref)

    far_ref[...] = chip_ref[pl.ds(jnp.where(ahead(2), blocks, 0), blocks + HALO)]


def pack(mine, other):
    total, rows, lanes = mine.shape
    blocks = total - HALO
    return pl.pallas_call(
        pack_kernel,
        out_shape=[
            jax.ShapeDtypeStruct((2 * blocks + HALO, rows, lanes), jnp.bfloat16),
            jax.ShapeDtypeStruct((blocks + HALO, rows, lanes), jnp.bfloat16),
        ],
        in_specs=[VMEM] * 2,
        out_specs=[VMEM] * 2,
        compiler_params=pltpu.CompilerParams(vmem_limit_bytes=8 * 2**20),
        name="pack",
    )(mine, other)


def couple_kernel(cols_ref, counts_ref, green_ref, chip_ref, near_ref, far_ref, swap_near_ref, swap_far_ref, out_ref, window):
    cols, counts = cols_ref[...], counts_ref[...]
    rows, lanes = chip_ref.shape[1:]
    blocks = far_ref.shape[0] - HALO
    angles = rows // 2
    entries = green_ref.shape[1]
    me = lax.axis_index("dom")

    def put(slot, ref, first, halo_ref=None, halo_first=None):
        at = slot * blocks
        if halo_ref is None:
            window[pl.ds(at, blocks)] = ref[pl.ds(first, blocks)]
            return
        low = ref[pl.ds(first, HALO)].astype(jnp.float32)
        halo = halo_ref[pl.ds(halo_first, HALO)].astype(jnp.float32)
        window[pl.ds(at, HALO)] = (low + halo).astype(window.dtype)
        window[pl.ds(at + HALO, blocks - HALO)] = ref[pl.ds(first + HALO, blocks - HALO)]

    def fill(left_ref, right_ref, left_far_ref, right_far_ref):
        put(0, left_far_ref, 0)
        put(1, left_ref, 0, left_far_ref, blocks)
        put(2, left_ref, blocks)
        put(3, chip_ref, 0, left_ref, 2 * blocks)
        put(4, chip_ref, blocks)
        put(5, right_ref, 0, chip_ref, 2 * blocks)
        put(6, right_ref, blocks)
        put(7, right_far_ref, 0, right_ref, 2 * blocks)

    for near_ahead, sides in ((True, (swap_near_ref, near_ref)), (False, (near_ref, swap_near_ref))):
        for far_ahead, far_sides in ((True, (swap_far_ref, far_ref)), (False, (far_ref, swap_far_ref))):

            @pl.when(jnp.logical_and(ahead(1) == near_ahead, ahead(2) == far_ahead))
            def _(sides=sides, far_sides=far_sides):
                fill(*sides, *far_sides)

    dead = 8 * blocks
    window[dead] = jnp.zeros((rows, lanes), window.dtype)
    first_col = (me - lax.rem(me, 2) - REACH) * blocks
    for r in range(green_ref.shape[0]):
        picked = []
        for k in range(entries):
            picked.append(window[jnp.where(k < counts[0, r], cols[r, k] - first_col, dead)])
        wave = jnp.concatenate(picked, axis=1)
        green = jnp.concatenate(
            [green_ref[r, :, 0].reshape(entries * lanes, lanes), green_ref[r, :, 1].reshape(entries * lanes, lanes)],
            axis=1,
        )
        product = jnp.dot(wave, green, preferred_element_type=jnp.float32)
        at = pl.ds(r * lanes, lanes)
        out_ref[0, :, at] = product[:angles, :lanes] - product[angles:, lanes:]
        out_ref[1, :, at] = product[:angles, lanes:] + product[angles:, :lanes]


def couple(block_cols, block_counts, green, chip, near, far, swap_near, swap_far):
    rows_here, entries = block_cols.shape
    _, rows, lanes = chip.shape
    blocks = far.shape[0] - HALO
    flops = rows_here * 2 * rows * entries * lanes * 2 * lanes
    return pl.pallas_call(
        couple_kernel,
        out_shape=jax.ShapeDtypeStruct((2, rows // 2, rows_here * lanes), jnp.float32),
        in_specs=[VMEM] * 8,
        out_specs=VMEM,
        scratch_shapes=[pltpu.VMEM((8 * blocks + 8, rows, lanes), jnp.bfloat16)],
        compiler_params=pltpu.CompilerParams(vmem_limit_bytes=24 * 2**20),
        cost_estimate=pl.CostEstimate(flops=flops, bytes_accessed=green.size * 2, transcendentals=0),
        name="couple",
    )(block_cols, block_counts[None], green, chip, near, far, swap_near, swap_far)


def per_device(incident, response, jitter, block_cols, block_counts, green_blocks):
    half = incident.shape[0] // 2
    low, high = incident[:half], incident[half:]
    one_low, two_high = angle_pairs(low, 0), angle_pairs(high, 1)
    one_high, two_low = angle_pairs(high, 0), angle_pairs(low, 1)
    (own,) = respond(jitter, response, [(low, high)], jnp.float32)
    one_low, two_high = gate(one_low, own), gate(two_high, own)
    across_low, across_high = angle_pairs(one_low, 1), angle_pairs(two_high, 0)

    one, two = respond(jitter, response, [(one_low, one_high), (two_low, two_high)])
    (across,) = respond(jitter, response, [(across_low, across_high)])
    mine = stitch([own, angle_pairs(one, 0), angle_pairs(two, 1), angle_pairs(across, 2)])

    chip, far = pack(mine, other_core(mine))
    near_in, far_in = pairs(chip, 1), pairs(far, 2)
    return couple(
        block_cols, block_counts, green_blocks, chip, near_in, far_in, other_core(near_in), other_core(far_in)
    )


def solution(mesh):
    return jax.shard_map(
        per_device,
        mesh=mesh,
        in_specs=(
            P("dom", None, "ang", None),
            P("dom", None, None, "ang"),
            P("dom"),
            P("dom", None),
            P("dom"),
            P("dom", None, None, None, None),
        ),
        out_specs=P(None, "ang", "dom"),
        check_vma=False,
    )
```

```python
import functools

import jax
import jax.numpy as jnp
from jax import lax
from jax.experimental import pallas as pl
from jax.experimental.pallas import tpu as pltpu
from jax.sharding import PartitionSpec as P

LANES = 128
REACH = 3
HALO = 4
VMEM = pl.BlockSpec(memory_space=pltpu.VMEM)
SMEM = pl.BlockSpec(memory_space=pltpu.SMEM)


def angle_pairs(block, shift):
    size = lax.axis_size("ang")
    if shift == 2:
        return lax.ppermute(block, "ang", [(a, (a + 2) % size) for a in range(size)])
    return lax.ppermute(block, "ang", [(a, (((a + shift) ^ 1) - shift) % size) for a in range(size)])


def other_core(block):
    doms = lax.axis_size("dom")
    return lax.ppermute(block, "dom", [(i, i ^ 1) for i in range(doms)])


def pairs(block, distance):
    chips = lax.axis_size("dom") // 2
    route = []
    for i in range(2 * chips):
        chip, core = i // 2, i % 2
        partner = chip ^ distance if core == distance - 1 else ((chip + distance) ^ distance) - distance
        if 0 <= partner < chips:
            route.append((i, 2 * partner + core))
    return lax.ppermute(block, "dom", route)


def ahead(distance):
    me = lax.axis_index("dom")
    return lax.rem(me + distance - 1, 2) == lax.rem(me // (2 * distance), 2)


def placed_sums(jitter_ref, pieces, response_ref):
    jitter = jitter_ref[...]
    domains = response_ref.shape[0]
    per_piece = domains // len(pieces)
    angles = pieces[0].shape[2]
    sums = [None] * (domains // 2 + 1)
    for d in range(domains):
        wave = pieces[d // per_piece][d % per_piece].reshape(2 * angles, -1)
        panel = jnp.concatenate([response_ref[d, 0], response_ref[d, 1]], axis=1)
        product = jnp.dot(wave, panel, preferred_element_type=jnp.float32)
        real = product[:angles, :LANES] - product[angles:, LANES:]
        imag = product[:angles, LANES:] + product[angles:, :LANES]
        field = jnp.concatenate([real, imag], axis=0).astype(jnp.bfloat16).astype(jnp.float32)
        start = (d % 2) * (LANES // 2) + jitter[0, d]
        turned = pltpu.roll(field, start, 1)
        lane = lax.broadcasted_iota(jnp.int32, turned.shape, 1)
        here = jnp.where(lane >= start, turned, 0.0)
        after = turned - here
        for block, part in ((d // 2, here), (d // 2 + 1, after)):
            sums[block] = part if sums[block] is None else sums[block] + part
    return sums


def gate_kernel(held_ref, after_ref, out_ref):
    pass


def gate(held, after):
    return pl.pallas_call(
        gate_kernel,
        out_shape=jax.ShapeDtypeStruct(held.shape, held.dtype),
        in_specs=[VMEM, VMEM],
        out_specs=VMEM,
        input_output_aliases={0: 0},
        compiler_params=pltpu.CompilerParams(vmem_limit_bytes=2**20),
        name="gate",
    )(held, after)


def respond_kernel(groups, halves, *refs):
    jitter_ref, response_ref = refs[0], refs[1]
    inputs = refs[2 : 2 + groups * halves]
    outputs = refs[2 + groups * halves :]
    for g in range(groups):
        sums = placed_sums(jitter_ref, inputs[g * halves : (g + 1) * halves], response_ref)
        for b, block in enumerate(sums):
            outputs[g][b] = block.astype(outputs[g].dtype)


def respond(jitter, response, groups, kind=jnp.bfloat16):
    domains, _, depth, cols = response.shape
    halves = len(groups[0])
    angles = groups[0][0].shape[2]
    sums = jax.ShapeDtypeStruct((domains // 2 + 1, 2 * angles, LANES), kind)
    return pl.pallas_call(
        functools.partial(respond_kernel, len(groups), halves),
        out_shape=[sums] * len(groups),
        in_specs=[VMEM, VMEM] + [VMEM] * (len(groups) * halves),
        out_specs=[VMEM] * len(groups),
        compiler_params=pltpu.CompilerParams(vmem_limit_bytes=16 * 2**20),
        cost_estimate=pl.CostEstimate(
            flops=len(groups) * domains * 8 * angles * depth * cols, bytes_accessed=2 * response.size, transcendentals=0
        ),
        name="respond",
    )(jitter[None], response, *[piece for group in groups for piece in group])


def stitch_kernel(*refs):
    sources, plane = refs[:4], refs[4]
    me = lax.axis_index("ang")
    plane[...] = jnp.zeros_like(plane)
    side = jnp.where(lax.rem(me, 2) == 0, 1, 3)
    for step, owner in enumerate((me, lax.rem(me + side, 4), lax.rem(me + 4 - side, 4), lax.rem(me + 2, 4))):
        plane[pl.ds(owner, sources[step].shape[0])] += sources[step][...].astype(jnp.float32)


def stitch(sources):
    blocks, rows, lanes = sources[0].shape
    return pl.pallas_call(
        stitch_kernel,
        out_shape=jax.ShapeDtypeStruct((blocks + 3, rows, lanes), jnp.float32),
        in_specs=[VMEM] * 4,
        out_specs=VMEM,
        compiler_params=pltpu.CompilerParams(vmem_limit_bytes=8 * 2**20),
        name="stitch",
    )(*sources)


def pack_kernel(mine_ref, other_ref, chip_ref, far_ref):
    odd = lax.rem(lax.axis_index("dom"), 2) == 1
    blocks = mine_ref.shape[0] - HALO

    def fill(even_ref, odd_ref):
        chip_ref[pl.ds(0, blocks)] = even_ref[pl.ds(0, blocks)].astype(chip_ref.dtype)
        joined = odd_ref[pl.ds(0, HALO)] + even_ref[pl.ds(blocks, HALO)]
        chip_ref[pl.ds(blocks, HALO)] = joined.astype(chip_ref.dtype)
        rest = odd_ref[pl.ds(HALO, blocks)]
        chip_ref[pl.ds(blocks + HALO, blocks)] = rest.astype(chip_ref.dtype)

    @pl.when(odd)
    def _():
        fill(other_ref, mine_ref)

    @pl.when(jnp.logical_not(odd))
    def _():
        fill(mine_ref, other_ref)

    far_ref[...] = chip_ref[pl.ds(jnp.where(ahead(2), blocks, 0), blocks + HALO)]


def pack(mine, other):
    total, rows, lanes = mine.shape
    blocks = total - HALO
    return pl.pallas_call(
        pack_kernel,
        out_shape=[
            jax.ShapeDtypeStruct((2 * blocks + HALO, rows, lanes), jnp.bfloat16),
            jax.ShapeDtypeStruct((blocks + HALO, rows, lanes), jnp.bfloat16),
        ],
        in_specs=[VMEM] * 2,
        out_specs=[VMEM] * 2,
        compiler_params=pltpu.CompilerParams(vmem_limit_bytes=8 * 2**20),
        name="pack",
    )(mine, other)


def couple_kernel(cols_ref, counts_ref, green_ref, chip_ref, near_ref, far_ref, swap_near_ref, swap_far_ref, out_ref, window):
    cols, counts = cols_ref[...], counts_ref[...]
    rows, lanes = chip_ref.shape[1:]
    blocks = far_ref.shape[0] - HALO
    angles = rows // 2
    entries = green_ref.shape[1]
    me = lax.axis_index("dom")

    def put(slot, ref, first, halo_ref=None, halo_first=None):
        at = slot * blocks
        if halo_ref is None:
            window[pl.ds(at, blocks)] = ref[pl.ds(first, blocks)]
            return
        low = ref[pl.ds(first, HALO)].astype(jnp.float32)
        halo = halo_ref[pl.ds(halo_first, HALO)].astype(jnp.float32)
        window[pl.ds(at, HALO)] = (low + halo).astype(window.dtype)
        window[pl.ds(at + HALO, blocks - HALO)] = ref[pl.ds(first + HALO, blocks - HALO)]

    def fill(left_ref, right_ref, left_far_ref, right_far_ref):
        put(0, left_far_ref, 0)
        put(1, left_ref, 0, left_far_ref, blocks)
        put(2, left_ref, blocks)
        put(3, chip_ref, 0, left_ref, 2 * blocks)
        put(4, chip_ref, blocks)
        put(5, right_ref, 0, chip_ref, 2 * blocks)
        put(6, right_ref, blocks)
        put(7, right_far_ref, 0, right_ref, 2 * blocks)

    for near_ahead, sides in ((True, (swap_near_ref, near_ref)), (False, (near_ref, swap_near_ref))):
        for far_ahead, far_sides in ((True, (swap_far_ref, far_ref)), (False, (far_ref, swap_far_ref))):

            @pl.when(jnp.logical_and(ahead(1) == near_ahead, ahead(2) == far_ahead))
            def _(sides=sides, far_sides=far_sides):
                fill(*sides, *far_sides)

    dead = 8 * blocks
    window[dead] = jnp.zeros((rows, lanes), window.dtype)
    first_col = (me - lax.rem(me, 2) - REACH) * blocks
    for r in range(green_ref.shape[0]):
        picked = []
        for k in range(entries):
            picked.append(window[jnp.where(k < counts[0, r], cols[r, k] - first_col, dead)])
        wave = jnp.concatenate(picked, axis=1)
        green = jnp.concatenate(
            [green_ref[r, :, 0].reshape(entries * lanes, lanes), green_ref[r, :, 1].reshape(entries * lanes, lanes)],
            axis=1,
        )
        product = jnp.dot(wave, green, preferred_element_type=jnp.float32)
        at = pl.ds(r * lanes, lanes)
        out_ref[0, :, at] = product[:angles, :lanes] - product[angles:, lanes:]
        out_ref[1, :, at] = product[:angles, lanes:] + product[angles:, :lanes]


def couple(block_cols, block_counts, green, chip, near, far, swap_near, swap_far):
    rows_here, entries = block_cols.shape
    _, rows, lanes = chip.shape
    blocks = far.shape[0] - HALO
    flops = rows_here * 2 * rows * entries * lanes * 2 * lanes
    return pl.pallas_call(
        couple_kernel,
        out_shape=jax.ShapeDtypeStruct((2, rows // 2, rows_here * lanes), jnp.float32),
        in_specs=[VMEM] * 8,
        out_specs=VMEM,
        scratch_shapes=[pltpu.VMEM((8 * blocks + 8, rows, lanes), jnp.bfloat16)],
        compiler_params=pltpu.CompilerParams(vmem_limit_bytes=24 * 2**20),
        cost_estimate=pl.CostEstimate(flops=flops, bytes_accessed=green.size * 2, transcendentals=0),
        name="couple",
    )(block_cols, block_counts[None], green, chip, near, far, swap_near, swap_far)


def per_device(incident, response, jitter, block_cols, block_counts, green_blocks):
    half = incident.shape[0] // 2
    low, high = incident[:half], incident[half:]
    one_low, two_high = angle_pairs(low, 0), angle_pairs(high, 1)
    one_high, two_low = angle_pairs(high, 0), angle_pairs(low, 1)
    (own,) = respond(jitter, response, [(low, high)], jnp.float32)
    one_low, two_high = gate(one_low, own), gate(two_high, own)
    across_low, across_high = angle_pairs(one_low, 1), angle_pairs(two_high, 0)

    (one,) = respond(jitter, response, [(one_low, one_high)])
    (two,) = respond(jitter, response, [(two_low, two_high)])
    (across,) = respond(jitter, response, [(across_low, across_high)])
    mine = stitch([own, angle_pairs(one, 0), angle_pairs(two, 1), angle_pairs(across, 2)])

    chip, far = pack(mine, other_core(mine))
    near_in, far_in = pairs(chip, 1), pairs(far, 2)
    return couple(
        block_cols, block_counts, green_blocks, chip, near_in, far_in, other_core(near_in), other_core(far_in)
    )


def solution(mesh):
    return jax.shard_map(
        per_device,
        mesh=mesh,
        in_specs=(
            P("dom", None, "ang", None),
            P("dom", None, None, "ang"),
            P("dom"),
            P("dom", None),
            P("dom"),
            P("dom", None, None, None, None),
        ),
        out_specs=P(None, "ang", "dom"),
        check_vma=False,
    )
```
